32 devices in a mesh: dp: 8 (over z, x), mp: 4 (over y, core).
Axes of the slice: x: 2, y: 2, z: 4, core: 2. Of those that a mesh axis runs over, the one named last changes fastest.
Arguments:
- block_input: float32 [24, 768, 1024], P('dp', 'mp'), may hold values from -6 to 6
- history: bfloat16 [4, 24, 768, 1024], P(None, 'dp', 'mp'), may hold values from -6 to 6
- doc_lengths: int32 [24, 8], P('dp'), may hold values from 1 to 512, 1024 in all within a row
- grad_next: float32 [24, 768, 1024], P('dp', 'mp'), may hold values from -6 to 6
- grad_block: float32 [24, 768, 1024], P('dp', 'mp'), may hold values from -6 to 6
- attn_norm_gain: float32 [768], P('mp'), may hold values from 0.5 to 1.5
- attn_norm_bias: float32 [768], P('mp'), may hold values from -1.25 to 1.25
- qkv_weight: float32 [3, 768, 768], P(None, None, 'mp'), may hold values from -0.21875 to 0.21875
- qkv_bias: float32 [3, 768], P(None, 'mp'), may hold values from -1.25 to 1.25
- out_weight: float32 [768, 768], P('mp'), may hold values from -1.25 to 1.25
- out_bias: float32 [768], P('mp'), may hold values from -1.25 to 1.25
- ffn_norm_gain: float32 [768], P('mp'), may hold values from 0.5 to 1.5
- ffn_norm_bias: float32 [768], P('mp'), may hold values from -1.25 to 1.25
- up_weight: float32 [768, 3072], P(None, 'mp'), may hold values from -0.21875 to 0.21875
- up_bias: float32 [3072], P('mp'), may hold values from -1.25 to 1.25
- down_weight: float32 [3072, 768], P('mp'), may hold values from -0.15625 to 0.15625
- down_bias: float32 [768], P('mp'), may hold values from -1.25 to 1.25
- mix_weights: float32 [5], replicated, may hold values from 0.1 to 0.6
Outputs:
- next_input: float32 [24, 768, 1024], P('dp', 'mp')
- block_output: float32 [24, 768, 1024], P('dp', 'mp')
- input_grad: float32 [24, 768, 1024], P('dp', 'mp')
- history_grad: float32 [4, 24, 768, 1024], P(None, 'dp', 'mp')
- grad_attn_gain: float32 [768], P('mp')
- grad_attn_bias: float32 [768], P('mp')
- grad_qkv_weight: float32 [3, 768, 768], P(None, None, 'mp')
- grad_qkv_bias: float32 [3, 768], P(None, 'mp')
- grad_out_weight: float32 [768, 768], P('mp')
- grad_out_bias: float32 [768], P('mp')
- grad_ffn_gain: float32 [768], P('mp')
- grad_ffn_bias: float32 [768], P('mp')
- grad_up_weight: float32 [768, 3072], P(None, 'mp')
- grad_up_bias: float32 [3072], P('mp')
- grad_down_weight: float32 [3072, 768], P('mp')
- grad_down_bias: float32 [768], P('mp')
- grad_mix: float32 [5], replicated
The draws below stay inside these ranges and needn't reach their ends.
Inputs may be any that keep to these rules, and one draw needn't show every extreme that they name: `doc_lengths`: in each row the first 7 entries are its documents' lengths in order and the last one is the padding at the row's end; each row sums to 1024, and its largest entry is 512.
All inputs are finite; a program needn't handle non-finite values.
Results may differ from the reference program's by a relative error of at most 0.012.
Values may be sent and summed in bfloat16 or wider, within the bound.
No kernel may reach another device: no remote copies, remote signals or barrier semaphores. Data moves between devices by JAX's collectives and lax.ppermute only.
A program may use at most 192 MiB of HBM per device.

```python
import math
import jax
import jax.numpy as jnp
import numpy as np
from jax import lax

D = 768
HEADS = 12
HD = 64
FF = 3072
LEN = 1024
DOCS = 8
MOSTDOC = 512
HIST = 4
ROWS = 24


def block_scale(key, extent, pieces, smallest, high):
    factor_of = 1.0
    for dim, blocks in pieces:
        steps = jax.random.uniform(jax.random.fold_in(jax.random.fold_in(key, 6), dim), (blocks,), jnp.float32, smallest / len(pieces), high / len(pieces))
        factor_of = factor_of * jnp.repeat(jnp.exp(steps), extent[dim] // blocks).reshape((-1,) + (1,) * (len(extent) - 1 - dim))
    return factor_of


def split_up(amount, total, most, slope):
    portions = [(1 << 20) // math.isqrt(rank ** slope) + 1 for rank in range(2, amount + 1)]
    surplus, holding = total - most - (amount - 1), [1] * (amount - 1)
    while surplus > 0:
        free = [i for i in range(amount - 1) if holding[i] < most]
        whole, remaining = sum([portions[i] for i in free]), surplus
        for i in free:
            more = min(most - holding[i], max(1, remaining * portions[i] // whole), surplus)
            holding[i] = holding[i] + more
            surplus = surplus - more
    return np.array([most] + holding)


def uneven_parts(rng, number_of, total, bound, lean):
    if number_of == 2:
        one = jax.random.randint(rng, (), max(1, total - bound), min(bound, total - 1) + 1)
        return jnp.stack([one, total - one])
    lengths = jnp.asarray(split_up(number_of, total, bound, lean), jnp.int32)
    pairs = (number_of - 1) // 2
    source_of, taker = lengths[1:1 + 2 * pairs:2], lengths[2:2 + 2 * pairs:2]
    room = jnp.minimum(source_of - 1, bound - taker)
    moved = jax.random.randint(jax.random.fold_in(rng, 1), (pairs,), 0, 1 << 20) % (room + 1)
    lengths = lengths.at[1:1 + 2 * pairs:2].set(source_of - moved).at[2:2 + 2 * pairs:2].set(taker + moved)
    return lengths[jax.random.permutation(jax.random.fold_in(rng, 2), number_of)]


def normal_values(stream_key, shape, deviation, bound, shards=(), held_as=jnp.bfloat16):
    result = deviation * jax.random.normal(stream_key, shape, jnp.float32)
    if shards:
        result = result * block_scale(stream_key, shape, shards, -0.22, 0.18)
    return jnp.clip(result, -bound, bound).astype(held_as)


def setup_inputs(seed: int = 0) -> dict:
    key_of = jax.random.split(jax.random.key(seed), 19)
    return {
        "block_input": normal_values(key_of[0], (ROWS, D, LEN), 1.0, 6.0, ((0, 8), (1, 4)), jnp.float32),
        "history": normal_values(key_of[1], (HIST, ROWS, D, LEN), 1.0, 6.0, ((1, 8), (2, 4))),
        "doc_lengths": jax.vmap(lambda own: uneven_parts(own, DOCS, LEN, MOSTDOC, 2))(jax.random.split(key_of[2], ROWS)).reshape((ROWS, DOCS)).astype(jnp.int32),
        "grad_next": normal_values(key_of[3], (ROWS, D, LEN), 1.0, 6.0, ((0, 8), (1, 4)), jnp.float32),
        "grad_block": normal_values(key_of[4], (ROWS, D, LEN), 1.0, 6.0, ((0, 8), (1, 4)), jnp.float32),
        "attn_norm_gain": jnp.clip(1.0 + 0.1 * jax.random.normal(key_of[5], (D,), jnp.float32), 0.5, 1.5),
        "attn_norm_bias": normal_values(key_of[6], (D,), 0.2, 1.25, ((0, 4),), jnp.float32),
        "qkv_weight": normal_values(key_of[7], (3, D, D), D ** -0.5, 0.21875, ((2, 4),), jnp.float32),
        "qkv_bias": normal_values(key_of[8], (3, D), 0.2, 1.25, ((1, 4),), jnp.float32),
        "out_weight": normal_values(key_of[9], (D, D), (D // 32) ** -0.5, 1.25, ((0, 4),), jnp.float32),
        "out_bias": normal_values(key_of[10], (D,), 0.2, 1.25, ((0, 4),), jnp.float32),
        "ffn_norm_gain": jnp.clip(1.0 + 0.1 * jax.random.normal(key_of[11], (D,), jnp.float32), 0.5, 1.5),
        "ffn_norm_bias": normal_values(key_of[12], (D,), 0.2, 1.25, ((0, 4),), jnp.float32),
        "up_weight": normal_values(key_of[13], (D, FF), D ** -0.5, 0.21875, ((1, 4),), jnp.float32),
        "up_bias": normal_values(key_of[14], (FF,), 0.2, 1.25, ((0, 4),), jnp.float32),
        "down_weight": normal_values(key_of[15], (FF, D), (FF // 2) ** -0.5, 0.15625, ((0, 4),), jnp.float32),
        "down_bias": normal_values(key_of[16], (D,), 0.2, 1.25, ((0, 4),), jnp.float32),
        "mix_weights": jnp.clip(jax.random.uniform(key_of[17], (HIST + 1,), jnp.float32, 0.1, 0.6), 0.1, 0.6),
    }


norm_eps = 1e-05

@jax.custom_vjp
def low(v):
    return lax.optimization_barrier(v.astype(jnp.bfloat16)).astype(jnp.float32)

@jax.custom_vjp
def low_back(v):
    return v

def low_keep(v):
    return (low(v), None)

def low_pass(kept, grad):
    return (grad,)

def back_keep(v):
    return (v, None)

def back_low(kept, grad):
    return (low(grad),)
low.defvjp(low_keep, low_pass)
low_back.defvjp(back_keep, back_low)

def doc_layout(doc_lengths, length):
    doc_ends = jnp.cumsum(doc_lengths, axis=1).astype(jnp.int32)
    doc_starts = doc_ends - doc_lengths
    places = jnp.arange(length, dtype=jnp.int32)
    segment = lax.optimization_barrier(jnp.sum((places[None, :, None] >= doc_ends[:, None, :]).astype(jnp.int32), axis=2))
    doc_count = doc_lengths.shape[1]
    member = segment[:, :, None] == jnp.arange(doc_count, dtype=jnp.int32)[None, None, :]
    begins = lax.optimization_barrier(jnp.sum(jnp.where(member, doc_starts[:, None, :], 0), axis=2)).astype(jnp.int32)
    return (segment, places[None, :] - begins, segment == doc_count - 1)

def rotary_tables(position, head_dim):
    half_dim = head_dim // 2
    inverse = 10000.0 ** (-jnp.arange(half_dim, dtype=jnp.float32) * 2.0 / head_dim)
    angles = position.astype(jnp.float32)[..., None] * inverse
    return (jnp.cos(angles), jnp.sin(angles))

def rotate(values, cosine, sine):
    half_dim = values.shape[-1] // 2
    leading = values[..., :half_dim]
    trailing = values[..., half_dim:]
    return jnp.concatenate([leading * cosine - trailing * sine, trailing * cosine + leading * sine], axis=-1)

def visible_block(segment, padding, first_row, last_row):
    places = jnp.arange(last_row, dtype=jnp.int32)
    query_places = places[first_row:last_row]
    same_doc = segment[first_row:last_row][:, None] == segment[:last_row][None, :]
    earlier = places[None, :] <= query_places[:, None]
    usable = jnp.logical_not(padding[:last_row])[None, :]
    return same_doc & earlier & usable | (places[None, :] == query_places[:, None])

def layer_norm(values, norm_gain, norm_bias):
    row_mean = lax.optimization_barrier(jnp.mean(values, axis=-1, keepdims=True))
    centered = values - row_mean
    row_var = lax.optimization_barrier(jnp.mean(centered * centered, axis=-1, keepdims=True))
    return centered * lax.rsqrt(row_var + norm_eps) * norm_gain + norm_bias

def attend_row(packed):
    queries, row_keys, row_values, visible_mask = packed
    highest = lax.Precision.HIGHEST
    scores = jnp.einsum('qhd,khd->hqk', queries, row_keys, precision=highest) * HD ** (-0.5)
    scores = jnp.where(visible_mask[None], low_back(scores), -1e+30)
    row_max = lax.optimization_barrier(jnp.max(scores, axis=2, keepdims=True))
    shifted_exp = jnp.exp(scores - row_max)
    probs = shifted_exp / lax.optimization_barrier(jnp.sum(shifted_exp, axis=2, keepdims=True))
    return jnp.einsum('hqk,khd->qhd', low(probs), row_values, precision=highest)

def forward(block_input, history, attn_norm_gain, attn_norm_bias, qkv_weight, qkv_bias, out_weight, out_bias, ffn_norm_gain, ffn_norm_bias, up_weight, up_bias, down_weight, down_bias, mix_weights, cosine, sine, visible_mask):
    highest = lax.Precision.HIGHEST
    row_count, length, full_width = block_input.shape
    normed_one = low(layer_norm(block_input, attn_norm_gain, attn_norm_bias))
    projected = jnp.einsum('rlc,sce->srle', normed_one, low(qkv_weight), precision=highest)
    projected = low_back(projected + qkv_bias[:, None, None, :])
    split = projected.reshape(3, row_count, length, HEADS, HD)
    queries = low(rotate(split[0], cosine, sine))
    row_keys = low(rotate(split[1], cosine, sine))
    row_values = low(split[2])
    attended = lax.map(jax.checkpoint(attend_row), (queries, row_keys, row_values, visible_mask))
    attended = low(low_back(attended.reshape(row_count, length, full_width)))
    mixed = jnp.einsum('rlc,ce->rle', attended, low(out_weight), precision=highest)
    hidden_state = block_input + low_back(mixed) + out_bias
    normed_two = low(layer_norm(hidden_state, ffn_norm_gain, ffn_norm_bias))
    pre_act = jnp.einsum('rlc,cf->rlf', normed_two, low(up_weight), precision=highest) + up_bias
    pre_act = low_back(pre_act)
    activated = low(jax.nn.gelu(pre_act, approximate=True))
    lowered = low_back(jnp.einsum('rlf,fe->rle', activated, low(down_weight), precision=highest))
    block_output = hidden_state + lowered + down_bias
    next_input = jnp.einsum('j,jrlc->rlc', mix_weights[:-1], history, precision=highest) + mix_weights[-1] * block_output
    return (next_input, block_output)

def reference(block_input, history, doc_lengths, grad_next, grad_block, attn_norm_gain, attn_norm_bias, qkv_weight, qkv_bias, out_weight, out_bias, ffn_norm_gain, ffn_norm_bias, up_weight, up_bias, down_weight, down_bias, mix_weights):
    block_input = jnp.swapaxes(block_input, 1, 2)
    history = jnp.swapaxes(history, 2, 3)
    grad_next = jnp.swapaxes(grad_next, 1, 2)
    grad_block = jnp.swapaxes(grad_block, 1, 2)
    row_count, length, full_width = block_input.shape
    segment, position, padding = doc_layout(doc_lengths, length)
    cosine, sine = rotary_tables(position, HD)
    cosine = cosine[:, :, None, :]
    sine = sine[:, :, None, :]

    def row_mask(seg_row, pad_row):
        return visible_block(seg_row, pad_row, 0, length)
    visible_mask = jax.vmap(row_mask)(segment, padding)
    live_mask = jnp.where(padding, 0.0, 1.0).astype(jnp.float32)[:, :, None]

    def wrapped(*params):
        return forward(*params, cosine, sine, visible_mask)
    params = (block_input, history.astype(jnp.float32), attn_norm_gain, attn_norm_bias, qkv_weight, qkv_bias, out_weight, out_bias, ffn_norm_gain, ffn_norm_bias, up_weight, up_bias, down_weight, down_bias, mix_weights)
    outputs, pullback = jax.vjp(wrapped, *params)
    grads = pullback((grad_next * live_mask, grad_block * live_mask))
    return (jnp.swapaxes(outputs[0], 1, 2), jnp.swapaxes(outputs[1], 1, 2), jnp.swapaxes(grads[0], 1, 2), jnp.swapaxes(grads[1], 2, 3), grads[2], grads[3], grads[4], grads[5], grads[6], grads[7], grads[8], grads[9], grads[10], grads[11], grads[12], grads[13], grads[14])
```

```python
from functools import partial

import jax
import jax.numpy as jnp
from jax import lax
from jax.experimental import pallas as pl
from jax.experimental.pallas import tpu as pltpu
from jax.sharding import PartitionSpec as P

HD = 64
MOSTDOC = 512
norm_eps = 1e-05
bf16 = jnp.bfloat16
f32 = jnp.float32


def dot(a, b, dims):
    return lax.dot_general(a, b, (dims, ((), ())), preferred_element_type=f32)


TN = ((0,), (0,))
NN = ((1,), (0,))
NT = ((1,), (1,))


def windows(length, block):
    reach = -(-(MOSTDOC - 1) // block) * block
    return [(q, max(0, q - reach), q + block) for q in range(0, length, block)]


def masked_scores(q_ref, k_ref, lo_ref, q0, k0, k1, block):
    scores = dot(k_ref[0, :, k0:k1], q_ref[0, :, q0 : q0 + block], TN) * HD ** (-0.5)
    places = lax.broadcasted_iota(jnp.int32, scores.shape, 0) + k0
    own = lax.broadcasted_iota(jnp.int32, scores.shape, 1) + q0
    seen = (places >= lo_ref[0, :, q0 : q0 + block]) & (places <= own)
    return jnp.where(seen, scores, -1e30)


def attend_kernel(q_ref, k_ref, v_ref, lo_ref, o_ref, log_ref, *, block):
    for q0, k0, k1 in windows(q_ref.shape[2], block):
        scores = masked_scores(q_ref, k_ref, lo_ref, q0, k0, k1, block)
        top = jnp.max(scores, axis=0, keepdims=True)
        weights = jnp.exp(scores - top)
        total = jnp.sum(weights, axis=0, keepdims=True)
        mixed = dot(v_ref[0, :, k0:k1], weights.astype(bf16), NN)
        o_ref[0, :, q0 : q0 + block] = (mixed / total).astype(bf16)
        log_ref[0, :, q0 : q0 + block] = top + jnp.log(total)


def attend_back_kernel(
    q_ref, k_ref, v_ref, lo_ref, do_ref, log_ref, dq_ref, dk_ref, dv_ref, *, block
):
    dk_ref[...] = jnp.zeros_like(dk_ref)
    dv_ref[...] = jnp.zeros_like(dv_ref)
    for q0, k0, k1 in windows(q_ref.shape[2], block):
        here = slice(q0, q0 + block)
        scores = masked_scores(q_ref, k_ref, lo_ref, q0, k0, k1, block)
        probs = jnp.exp(scores - log_ref[0, :, here])
        grad_probs = dot(v_ref[0, :, k0:k1], do_ref[0, :, here], TN)
        crossed = probs * grad_probs
        total = jnp.sum(crossed, axis=0, keepdims=True)
        grad_scores = (crossed - probs * total).astype(bf16)
        probs = probs.astype(bf16)
        dq_ref[0, :, here] = dot(k_ref[0, :, k0:k1], grad_scores, NN) * HD ** (-0.5)
        dk_ref[0, :, k0:k1] += dot(q_ref[0, :, here], grad_scores, NT) * HD ** (-0.5)
        dv_ref[0, :, k0:k1] += dot(do_ref[0, :, here], probs, NT)


def head_spec(length):
    return pl.BlockSpec((1, HD, length), lambda h: (h, 0, 0))


def attend(queries, row_keys, row_values, low_end):
    heads, _, length = queries.shape
    block = min(256, length)
    line = pl.BlockSpec((1, 1, length), lambda h: (0, 0, 0))
    one = pl.BlockSpec((1, 1, length), lambda h: (h, 0, 0))
    cube = head_spec(length)
    return pl.pallas_call(
        partial(attend_kernel, block=block),
        grid=(heads,),
        in_specs=[cube, cube, cube, line],
        out_specs=[cube, one],
        out_shape=[
            jax.ShapeDtypeStruct(queries.shape, bf16),
            jax.ShapeDtypeStruct((heads, 1, length), f32),
        ],
        name="attend",
        cost_estimate=pl.CostEstimate(
            flops=4 * heads * HD * length * 600,
            transcendentals=heads * length * 600,
            bytes_accessed=8 * heads * HD * length,
        ),
    )(queries, row_keys, row_values, low_end)


def attend_back(queries, row_keys, row_values, low_end, grad_rows, log_sums):
    heads, _, length = queries.shape
    block = min(256, length)
    line = pl.BlockSpec((1, 1, length), lambda h: (0, 0, 0))
    one = pl.BlockSpec((1, 1, length), lambda h: (h, 0, 0))
    cube = head_spec(length)
    return pl.pallas_call(
        partial(attend_back_kernel, block=block),
        grid=(heads,),
        in_specs=[cube, cube, cube, line, cube, one],
        out_specs=[cube, cube, cube],
        out_shape=[jax.ShapeDtypeStruct(queries.shape, f32)] * 3,
        name="attend_back",
        cost_estimate=pl.CostEstimate(
            flops=10 * heads * HD * length * 600,
            transcendentals=heads * length * 600,
            bytes_accessed=20 * heads * HD * length,
        ),
    )(queries, row_keys, row_values, low_end, grad_rows, log_sums)


def swap(values, step, axis="mp"):
    size = lax.axis_size(axis)
    return lax.ppermute(values, axis, [(i, i ^ step) for i in range(size)])


ORDER = (0, 2, 1, 3)


def place_of(step):
    return ((step & 1) << 1) | (step >> 1)


def near_first(values, axis):
    me = lax.axis_index("mp")
    block = values.shape[axis] // 4
    return jnp.concatenate(
        [lax.dynamic_slice_in_dim(values, (me ^ s) * block, block, axis) for s in ORDER], axis
    )


def true_order(values, axis):
    me = lax.axis_index("mp")
    block = values.shape[axis] // 4
    return jnp.concatenate(
        [
            lax.dynamic_slice_in_dim(values, place_of(me ^ k) * block, block, axis)
            for k in range(4)
        ],
        axis,
    )


def gather_width(own):
    pair = jnp.concatenate([own, swap(own, 2)], axis=0)
    return jnp.concatenate([pair, swap(pair, 1)], axis=0)


def sum_width(parts):
    half = parts.shape[0] // 2
    near = parts[:half] + swap(parts[half:].astype(bf16), 1).astype(f32)
    block = half // 2
    return near[:block] + swap(near[block:].astype(bf16), 2).astype(f32)


def sum_small(values):
    near = values + swap(values, 1)
    return near + swap(near, 2)


def dp_steps():
    size, step = lax.axis_size("dp"), 1
    while step < size:
        yield step
        step *= 2


def sum_small_dp(values):
    for step in dp_steps():
        values = values + swap(values, step, "dp")
    return values


def sum_rows_dp(values):
    me = lax.axis_index("dp")
    steps = list(dp_steps())
    for step in steps:
        half = values.shape[0] // 2
        bit = (me // step) % 2
        kept = lax.dynamic_slice_in_dim(values, bit * half, half, 0)
        sent = lax.dynamic_slice_in_dim(values, (1 - bit) * half, half, 0)
        values = kept + swap(sent.astype(bf16), step, "dp").astype(f32)
    values = values.astype(bf16)
    for step in reversed(steps):
        bit = (me // step) % 2
        got = swap(values, step, "dp")
        both = jnp.concatenate([values, got, values], axis=0)
        values = lax.dynamic_slice_in_dim(both, bit * got.shape[0], 2 * got.shape[0], 0)
    return values


def doc_layout(doc_lengths, length):
    ends = jnp.cumsum(doc_lengths, axis=1)
    starts = ends - doc_lengths
    places = jnp.arange(length, dtype=jnp.int32)
    inside = (places >= starts[:, :, None]) & (places < ends[:, :, None])
    begins = jnp.sum(jnp.where(inside, starts[:, :, None], 0), axis=1)
    padding = places[None, :] >= starts[:, -1:]
    return begins, padding


def rotary_tables(position, head_dim):
    half = head_dim // 2
    inverse = 10000.0 ** (-jnp.arange(half, dtype=f32) * 2.0 / head_dim)
    angles = position.astype(f32)[:, None, :] * inverse[None, :, None]
    return jnp.cos(angles), jnp.sin(angles)


def rotate(values, cosine, sine):
    half = values.shape[1] // 2
    a, b = values[:, :half], values[:, half:]
    return jnp.concatenate([a * cosine - b * sine, b * cosine + a * sine], axis=1)


def sums_of(first, second):
    return jnp.stack([jnp.sum(first, axis=0), jnp.sum(second, axis=0)])


def unitize(values, sums, width):
    mean = sums[0] / width
    inverse = lax.rsqrt(sums[1] / width - mean * mean + norm_eps)
    return (values - mean) * inverse, inverse


def norm_back(gradient, unit, inverse, gain, width):
    weighted = gradient * gain
    sums = sum_small(sums_of(weighted, weighted * unit)) / width
    return inverse * (weighted - sums[0] - unit * sums[1])


def gelu_parts(v):
    c = 0.7978845608028654
    t = jnp.tanh(c * (v + 0.044715 * v * v * v))
    slope = 0.5 * (1.0 + t) + 0.5 * v * (1.0 - t * t) * c * (1.0 + 3 * 0.044715 * v * v)
    return 0.5 * v * (1.0 + t), slope


def shards(
    block_input, history, doc_lengths, grad_next, grad_block, attn_gain, attn_bias, qkv_weight,
    qkv_bias, out_weight, out_bias, ffn_gain, ffn_bias, up_weight, up_bias, down_weight,
    down_bias, mix,
):
    rows, local, length = block_input.shape
    width = qkv_weight.shape[1]
    heads = local // HD
    begins, padding = doc_layout(doc_lengths, length)
    places = jnp.arange(length, dtype=jnp.int32)
    cosine, sine = rotary_tables(places - begins, HD)
    low_end = jnp.where(padding, places, begins)[:, None, :]
    live = jnp.where(padding, 0.0, 1.0).astype(f32)
    col = lambda v: v[:, None]
    each = range(rows)

    sums = sum_small(
        jnp.stack([jnp.sum(block_input, axis=1), jnp.sum(block_input * block_input, axis=1)])
    )
    qkv_cols = near_first(
        jnp.concatenate([qkv_weight[s] for s in range(3)], axis=1).astype(bf16), 0
    )
    out_cols = near_first(out_weight.astype(bf16), 1)
    up_rows = near_first(up_weight.astype(bf16), 0)
    down_cols = near_first(down_weight.astype(bf16), 1)
    qkv_line = qkv_bias.reshape(3 * local, 1)

    unit_one, inv_one, full_one, grad_y, grad_full = [], [], [], [], []
    for r in each:
        unit, inverse = unitize(block_input[r], sums[:, r], width)
        unit_one.append(unit)
        inv_one.append(inverse)
        full_one.append(gather_width((unit * col(attn_gain) + col(attn_bias)).astype(bf16)))
    for r in each:
        grad_y.append((grad_block[r] + mix[-1] * grad_next[r]) * live[r])
        grad_full.append(gather_width(grad_y[r].astype(bf16)))

    packed, attended, logs, hidden, unit_two, inv_two, full_two = [], [], [], [], [], [], []
    for r in each:
        pre = (dot(qkv_cols, full_one[r], TN) + qkv_line).reshape(3, heads, HD, length)
        q = rotate(pre[0], cosine[r], sine[r]).astype(bf16)
        k = rotate(pre[1], cosine[r], sine[r]).astype(bf16)
        packed.append((q, k, pre[2].astype(bf16), low_end[r : r + 1]))
        o, log_sums = attend(*packed[r])
        attended.append(o.reshape(local, length))
        logs.append(log_sums)
        mixed = sum_width(dot(out_cols, attended[r], TN))
        hidden.append(block_input[r] + mixed + col(out_bias))
        unit, inverse = unitize(hidden[r], sum_small(sums_of(hidden[r], hidden[r] ** 2)), width)
        unit_two.append(unit)
        inv_two.append(inverse)
        full_two.append(gather_width((unit * col(ffn_gain) + col(ffn_bias)).astype(bf16)))

    block_out, next_in, grad_hidden, grad_pres, acts = [], [], [], [], []
    grad_hidden_full, grad_two = [], []
    for r in each:
        pre = dot(up_rows, full_two[r], TN) + col(up_bias)
        act, slope = gelu_parts(pre)
        acts.append(act.astype(bf16))
        grad_pres.append((dot(down_cols, grad_full[r], NN) * slope).astype(bf16))
        normed = sum_width(dot(up_rows, grad_pres[r], NN))
        grad_two.append(normed)
        lowered = sum_width(dot(down_cols, acts[r], TN))
        block_out.append(hidden[r] + lowered + col(down_bias))
        grad_hidden.append(
            grad_y[r] + norm_back(normed, unit_two[r], inv_two[r], col(ffn_gain), width)
        )
        grad_hidden_full.append(gather_width(grad_hidden[r].astype(bf16)))

    def over_rows(left, right):
        return sum(dot(left[r], right[r], NT) for r in each)

    ffn_grads = sum_rows_dp(
        jnp.concatenate([over_rows(acts, grad_full), over_rows(grad_pres, full_two)])
    )

    grad_qkv, grad_one, input_grad = [], [], []
    for r in each:
        grad_att = dot(out_cols, grad_hidden_full[r], NN).astype(bf16)
        dq, dk, dv = attend_back(*packed[r], grad_att.reshape(heads, HD, length), logs[r])
        turned = [rotate(dq, cosine[r], -sine[r]), rotate(dk, cosine[r], -sine[r]), dv]
        grad_qkv.append(jnp.stack(turned).reshape(3 * local, length).astype(bf16))
        normed = sum_width(dot(qkv_cols, grad_qkv[r], NN))
        grad_one.append(normed)
        input_grad.append(
            grad_hidden[r] + norm_back(normed, unit_one[r], inv_one[r], col(attn_gain), width)
        )
    attn_grads = sum_rows_dp(
        jnp.concatenate([over_rows(attended, grad_hidden_full), over_rows(grad_qkv, full_one)])
    )

    grad_out = grad_next * live[:, None, :]
    hist = history.astype(f32)
    block_output = jnp.stack(block_out)
    next_input = jnp.sum(mix[:-1, None, None, None] * hist, axis=0) + mix[-1] * block_output
    history_grad = mix[:-1, None, None, None] * grad_out[None]
    mix_terms = jnp.concatenate(
        [jnp.sum(hist * grad_out[None], axis=(1, 2, 3)), jnp.sum(block_output * grad_out)[None]]
    )

    def tokens(parts):
        return sum(jnp.sum(p.astype(f32), axis=1) for p in parts)

    small = [
        tokens([grad_one[r] * unit_one[r] for r in each]),
        tokens(grad_one),
        tokens(grad_qkv),
        tokens(grad_hidden),
        tokens([grad_two[r] * unit_two[r] for r in each]),
        tokens(grad_two),
        tokens(grad_pres),
        tokens(grad_y),
        sum_small(mix_terms),
    ]
    summed = sum_small_dp(jnp.concatenate(small))
    cuts, at = [], 0
    for part in small:
        cuts.append(summed[at : at + part.shape[0]])
        at += part.shape[0]
    ffn_grads = true_order(ffn_grads, 1)
    attn_grads = true_order(attn_grads, 1)
    ff = up_bias.shape[0]
    return (
        next_input,
        block_output,
        jnp.stack(input_grad),
        history_grad,
        cuts[0],
        cuts[1],
        jnp.swapaxes(attn_grads[local:].reshape(3, local, width), 1, 2).astype(f32),
        cuts[2].reshape(3, local),
        attn_grads[:local].astype(f32),
        cuts[3],
        cuts[4],
        cuts[5],
        ffn_grads[ff:].T.astype(f32),
        cuts[6],
        ffn_grads[:ff].astype(f32),
        cuts[7],
        cuts[8],
    )


def solution(mesh):
    placed = (
        P("dp", "mp", None),
        P(None, "dp", "mp", None),
        P("dp", None),
        P("dp", "mp", None),
        P("dp", "mp", None),
        P("mp"),
        P("mp"),
        P(None, None, "mp"),
        P(None, "mp"),
        P("mp", None),
        P("mp"),
        P("mp"),
        P("mp"),
        P(None, "mp"),
        P("mp"),
        P("mp", None),
        P("mp"),
        P(),
    )
    return jax.shard_map(
        shards,
        mesh=mesh,
        in_specs=placed,
        out_specs=(
            P("dp", "mp", None),
            P("dp", "mp", None),
            P("dp", "mp", None),
            P(None, "dp", "mp", None),
            P("mp"),
            P("mp"),
            P(None, None, "mp"),
            P(None, "mp"),
            P("mp", None),
            P("mp"),
            P("mp"),
            P("mp"),
            P(None, "mp"),
            P("mp"),
            P("mp", None),
            P("mp"),
            P(),
        ),
        check_vma=False,
    )
```
